32 devices in a mesh: va: 8 (over y, x, core), vb: 4 (over z).
Axes of the slice: x: 2, y: 2, z: 4, core: 2. Of those that a mesh axis runs over, the one named last changes fastest.
Arguments:
- clique_a: float32 [16, 8, 2, 16, 32768], P('va', 'vb'), may hold values from 0.2 to 5
- message_in: float32 [16, 2, 32768], P('va'), may hold values from 0.2 to 5
- clique_b: float32 [32, 8, 16, 16, 8, 256], P(None, None, None, 'va', 'vb'), may hold values from 0.2 to 5
- old_separator: float32 [8, 16, 16, 8, 256], P(None, None, 'va', 'vb'), may hold values from 0.25 to 4
Outputs:
- absorbed: float32 [16, 8, 2, 16, 32768], P('va', 'vb')
- updated_b: float32 [32, 8, 16, 16, 8, 256], P(None, None, None, 'va', 'vb')
- onward: float32 [32, 16, 16, 256], P('vb', None, 'va')
The draws below stay inside these ranges and needn't reach their ends.
All inputs are finite; a program needn't handle non-finite values.
Results may differ from the reference program's by a relative error of at most 0.00002.
Values sent between devices are 32-bit elements; how exact they have to be, the bound alone decides.
No kernel may reach another device: no remote copies, remote signals or barrier semaphores. Data moves between devices by JAX's collectives and lax.ppermute only.
A program may use at most 192 MiB of HBM per device.

```python
import math
import jax
import jax.numpy as jnp

H = 16
K = 2
P_SIZE = 8
Q = 16
R1 = 16
R2 = 8
R3 = 256
E = 32
R = 32768


def block_levels(own_key, extent, cuts, low, largest):
    gain, own = 1.0, jax.random.fold_in(own_key, 6)
    for axis_at, blocks in cuts:
        draws = jnp.exp(jax.random.uniform(jax.random.fold_in(own, axis_at), (blocks,), jnp.float32, low / len(cuts), largest / len(cuts)))
        gain = gain * jnp.repeat(draws, extent[axis_at] // blocks).reshape([-1 if axis == axis_at else 1 for axis in range(len(extent))])
    return gain


def setup_inputs(seed: int = 0) -> dict:
    keys = jax.random.split(jax.random.key(seed), 5)
    return {
        "clique_a": jnp.clip(jnp.exp(math.log(5.0) - 3.218876 * jax.random.uniform(keys[0], (H, P_SIZE, K, Q, R), jnp.float32) ** block_levels(keys[0], (H, P_SIZE, K, Q, R), ((0, 8), (1, 4)), -0.2, 0.2)), 0.2, 5.0),
        "message_in": jnp.clip(jnp.exp(math.log(5.0) - 3.218876 * jax.random.uniform(keys[1], (H, K, R), jnp.float32) ** block_levels(keys[1], (H, K, R), ((0, 8),), -0.2, 0.2)), 0.2, 5.0),
        "clique_b": jnp.clip(jnp.exp(math.log(5.0) - 3.218876 * jax.random.uniform(keys[2], (E, P_SIZE, Q, R1, R2, R3), jnp.float32) ** block_levels(keys[2], (E, P_SIZE, Q, R1, R2, R3), ((3, 8), (4, 4)), -0.2, 0.2)), 0.2, 5.0),
        "old_separator": jnp.clip(jnp.exp(math.log(4.0) - 2.7725887 * jax.random.uniform(keys[3], (P_SIZE, Q, R1, R2, R3), jnp.float32) ** block_levels(keys[3], (P_SIZE, Q, R1, R2, R3), ((2, 8), (3, 4)), -0.2, 0.2)), 0.25, 4.0),
    }


def reference(clique_a, message_in, clique_b, old_separator):
    absorbed = clique_a * message_in[:, None, :, None, :]
    separator = jnp.sum(absorbed, axis=(0, 2)) * (1.0 / (H * K))
    separator = separator.reshape(P_SIZE, Q, R1, R2, R3)
    updated_b = clique_b * (separator / old_separator)[None]
    onward = jnp.sum(updated_b, axis=(1, 4)) * (1.0 / (P_SIZE * R2))
    return absorbed, updated_b, onward
```

```python
import functools

import jax
import jax.numpy as jnp
from jax import lax
from jax.experimental import pallas as pl
from jax.experimental.pallas import tpu as pltpu
from jax.sharding import PartitionSpec as P

H = 16
K = 2
P_SIZE = 8
R1 = 16
R2 = 8
R3 = 256
LANES = 128
QT = 8


def generic_body(clique_a, message_in, clique_b, old_separator):
    p_local = clique_a.shape[1]
    q_total = clique_a.shape[3]
    r_total = clique_a.shape[4]
    absorbed = clique_a * message_in[:, None, :, None, :]
    column_width = r_total // R1
    summed = jnp.sum(absorbed, axis=(0, 2)) * (1.0 / (H * K))
    summed = summed.reshape(
        p_local, q_total, lax.axis_size("va") * (R1 // lax.axis_size("va")), column_width
    )
    shares = lax.psum_scatter(
        jnp.transpose(summed, (2, 0, 1, 3)), "va", scatter_dimension=0, tiled=True
    )
    shares = shares.reshape(shares.shape[0], p_local, q_total, R2, R3)
    moved = lax.all_to_all(shares, "vb", split_axis=3, concat_axis=1, tiled=True)
    separator = jnp.transpose(moved, (1, 2, 0, 3, 4))
    scaling = separator / old_separator
    updated_b = clique_b * scaling[None]
    partial_value = jnp.sum(updated_b, axis=(1, 4)) * (1.0 / (P_SIZE * R2))
    onward = lax.psum_scatter(partial_value, "vb", scatter_dimension=0, tiled=True)
    return (absorbed, updated_b, onward)


def swap(x, axis, mask):
    n = lax.axis_size(axis)
    return lax.ppermute(x, axis, [(i, i ^ mask) for i in range(n)])


def absorb_kernel(tab_ref, a_ref, m_ref, *rest):
    o_ref, s_ref = rest[-2:]
    nh, npl, nk = a_ref.shape[:3]
    nm, nr1, width = s_ref.shape[2], s_ref.shape[3], s_ref.shape[5]
    for r1 in range(nr1):
        for m in range(nm):
            block = tab_ref[1 + m]
            off = pl.multiple_of(r1 * (nm * width) + block * width, width)
            lanes = pl.ds(off, width)
            msg = [
                [jnp.broadcast_to(m_ref[h, pl.ds(k, 1), lanes], (QT, width)) for k in range(nk)]
                for h in range(nh)
            ]
            for p in range(npl):
                total = None
                for h in range(nh):
                    for k in range(nk):
                        value = a_ref[h, p, k, :, lanes] * msg[h][k]
                        o_ref[h, p, k, :, lanes] = value
                        total = value if total is None else total + value
                s_ref[0, p, m, r1] = total


def absorb(tab, clique_a, message, absorbed, chunk, part, n_va, n_vb):
    nh, npl, nk, nq, nr = clique_a.shape
    block = nr // n_va
    nr1 = R1 // n_va
    width = block // nr1 // n_vb
    steps = n_va // 2
    a_spec = pl.BlockSpec(
        (nh, npl, nk, QT, block), lambda g, t: (0, 0, 0, chunk, t[0] ^ (2 * g + part))
    )
    in_specs = [
        a_spec,
        pl.BlockSpec((nh, nk, block), lambda g, t: (0, 0, t[0] ^ (2 * g + part))),
    ]
    args = [tab, clique_a, message]
    aliases = {}
    if absorbed is not None:
        in_specs.append(pl.BlockSpec(memory_space=pl.ANY))
        args.append(absorbed)
        aliases = {3: 0}
    piece = (npl, n_vb, nr1, QT, width)
    n_a = nh * npl * nk * QT * block * steps
    return pl.pallas_call(
        absorb_kernel,
        grid_spec=pltpu.PrefetchScalarGridSpec(
            num_scalar_prefetch=1,
            grid=(steps,),
            in_specs=in_specs,
            out_specs=[a_spec, pl.BlockSpec((1,) + piece, lambda g, t: (g, 0, 0, 0, 0, 0))],
        ),
        out_shape=[
            jax.ShapeDtypeStruct(clique_a.shape, clique_a.dtype),
            jax.ShapeDtypeStruct((steps,) + piece, clique_a.dtype),
        ],
        input_output_aliases=aliases,
        cost_estimate=pl.CostEstimate(flops=2 * n_a, bytes_accessed=9 * n_a, transcendentals=0),
        name="absorb",
    )(*args)


def update_kernel(n_pieces, tab_ref, b_ref, old_ref, *rest):
    seps = rest[:n_pieces]
    u_ref, on_ref, scale, col = rest[-4:]
    step = pl.program_id(0)
    npl, nr1, _, width = seps[0].shape
    nhi = R3 // LANES
    nr2 = width // R3
    tile = nr1 * nhi * nr2

    @pl.when(step == 0)
    def _():
        for m in range(n_pieces):
            for p in range(npl):
                row = tab_ref[1 + m] * npl + p
                for r1 in range(nr1):
                    for r2 in range(nr2):
                        for hi in range(nhi):
                            at = (r2 * nhi + hi) * LANES
                            scale[row, pl.ds((r1 * nhi + hi) * nr2 + r2, QT, stride=tile), :] = (
                                seps[m][p, r1, :, at : at + LANES]
                            )
        scale[...] = scale[...] * (1.0 / (H * K)) / old_ref[...]

    ne, npt = b_ref.shape[:2]
    rows = b_ref.shape[2]
    for e in range(ne):
        total = None
        for p in range(npt):
            value = b_ref[e, p] * scale[p]
            u_ref[e, p] = value
            total = value if total is None else total + value
        col[e] = total * (1.0 / (P_SIZE * R2))
        for hi in range(nhi):
            for r1 in range(nr1):
                acc = None
                for r2 in range(nr2):
                    piece = col[e, pl.ds((r1 * nhi + hi) * nr2 + r2, QT, stride=tile), :]
                    acc = piece if acc is None else acc + piece
                on_ref[0, e, pl.ds(hi * nr1 + r1, QT, stride=nhi * nr1), :] = acc


def update(tab, clique_b, old, seps, updated, chunk, order, n_vb):
    ne, npt, rows, _ = clique_b.shape
    crow = QT * (rows // (clique_b.shape[2] // 8))
    rows_c = 8 * QT
    orow = rows_c // 2
    be = ne // n_vb // 2
    npc = len(order)

    def at(g, t):
        return t[1 + n_vb + g]

    b_spec = pl.BlockSpec((be, npt, rows_c, LANES), lambda g, t: (at(g, t), 0, chunk, 0))
    in_specs = [
        b_spec,
        pl.BlockSpec((npt, rows_c, LANES), lambda g, t: (0, chunk, 0)),
    ] + [pl.BlockSpec(s.shape, lambda g, t: (0, 0, 0, 0)) for s in seps]
    z = tab[1]
    tab = jnp.concatenate([tab[: 1 + n_vb], jnp.stack([(z ^ m) * 2 + half for m, half in order])])
    args = [tab, clique_b, old, *seps]
    aliases = {}
    if updated is not None:
        in_specs.append(pl.BlockSpec(memory_space=pl.ANY))
        args.append(updated)
        aliases = {len(args) - 1: 0}
    n_b = be * npt * rows_c * LANES * npc
    return pl.pallas_call(
        functools.partial(update_kernel, len(seps)),
        grid_spec=pltpu.PrefetchScalarGridSpec(
            num_scalar_prefetch=1,
            grid=(npc,),
            in_specs=in_specs,
            out_specs=[
                b_spec,
                pl.BlockSpec((1, be, orow, LANES), lambda g, t: (g, 0, 0, 0)),
            ],
            scratch_shapes=[
                pltpu.VMEM((npt, rows_c, LANES), jnp.float32),
                pltpu.VMEM((be, rows_c, LANES), jnp.float32),
            ],
        ),
        out_shape=[
            jax.ShapeDtypeStruct(clique_b.shape, clique_b.dtype),
            jax.ShapeDtypeStruct((npc, be, orow, LANES), clique_b.dtype),
        ],
        input_output_aliases=aliases,
        cost_estimate=pl.CostEstimate(flops=2 * n_b, bytes_accessed=8 * n_b, transcendentals=0),
        name="update",
    )(*args)


def body(clique_a, message_in, clique_b, old_separator):
    n_va, n_vb = lax.axis_size("va"), lax.axis_size("vb")
    npl, nq = clique_a.shape[1], clique_a.shape[3]
    ne, npt, _, nr1, nr2, _ = clique_b.shape
    nhi = R3 // LANES
    n_chunks = nq // QT

    me, z = lax.axis_index("va"), lax.axis_index("vb")
    tab = jnp.stack([me] + [z ^ m for m in range(n_vb)]).astype(jnp.int32)

    def rows_view(x):
        lead = x.shape[:-3]
        x = x.reshape(lead + (nr1, nr2, nhi, LANES))
        n = len(lead)
        x = jnp.swapaxes(x, n + 1, n + 2)
        return x.reshape(lead[:-1] + (lead[-1] * nr1 * nhi * nr2, LANES))

    b_rows, old_rows = rows_view(clique_b), rows_view(old_separator)

    absorbed, seps = None, []
    for c in range(n_chunks):
        absorbed, send = absorb(tab, clique_a, message_in, absorbed, c, 1, n_va, n_vb)
        got = swap(send, "va", 1)
        absorbed, keep = absorb(tab, clique_a, message_in, absorbed, c, 0, n_va, n_vb)
        keep = keep.reshape((2, 2) + keep.shape[1:])
        got = got.reshape(keep.shape)
        x0 = keep[:, 1, 0] + got[:, 1, 0]
        y1 = keep[1, :, 1] + got[1, :, 1]
        x0, y1 = swap(x0, "va", 2), swap(y1, "va", 4)
        y0 = keep[1, 0, 0] + got[1, 0, 0] + x0[1]
        x1 = keep[0, 1, 1] + got[0, 1, 1] + y1[1]
        k0 = keep[0, 0, 0] + got[0, 0, 0] + x0[0]
        k1 = keep[0, 0, 1] + got[0, 0, 1] + y1[0]
        y0, x1 = swap(y0, "va", 4), swap(x1, "va", 2)
        pieces = [jnp.stack([k0[m] + y0[m], k1[m] + x1[m]]) for m in range(n_vb)]
        seps.append([pieces[0]] + [swap(pieces[m], "vb", m) for m in range(1, n_vb)])

    updated, onward = None, []
    for c in range(n_chunks):
        send_order = [(1, 0), (2, 0), (3, 1), (2, 1)]
        keep_order = [(0, 0), (3, 0), (0, 1), (1, 1)]
        updated, send = update(tab, b_rows, old_rows, seps[c], updated, c, send_order, n_vb)
        g0, g1 = swap(send[:2], "vb", 1), swap(send[2:], "vb", 3)
        updated, keep = update(tab, b_rows, old_rows, seps[c], updated, c, keep_order, n_vb)
        s0, s1 = keep[1] + g0[1], keep[3] + g1[1]
        k0, k1 = keep[0] + g0[0], keep[2] + g1[0]
        s0, s1 = swap(s0, "vb", 3), swap(s1, "vb", 1)
        onward.append(jnp.concatenate([k0 + s0, k1 + s1], axis=0))

    e_out = ne // n_vb
    onward = jnp.concatenate(
        [o.reshape(e_out, QT, nhi, nr1, LANES) for o in onward], axis=1
    )
    onward = jnp.swapaxes(onward, 2, 3).reshape(e_out, nq, nr1, R3)
    updated = updated.reshape(ne, npt, nq, nr1, nhi, nr2, LANES)
    updated = jnp.swapaxes(updated, 4, 5).reshape(clique_b.shape)
    return (absorbed, updated, onward)


def solution(mesh):
    small = mesh.shape["va"] == 8 and mesh.shape["vb"] == 4
    return jax.shard_map(
        body if small else generic_body,
        mesh=mesh,
        in_specs=(
            P("va", "vb", None, None, None),
            P("va", None, None),
            P(None, None, None, "va", "vb", None),
            P(None, None, "va", "vb", None),
        ),
        out_specs=(
            P("va", "vb", None, None, None),
            P(None, None, None, "va", "vb", None),
            P("vb", None, "va", None),
        ),
        check_vma=False,
    )
```

```python
import functools

import jax
import jax.numpy as jnp
from jax import lax
from jax.experimental import pallas as pl
from jax.experimental.pallas import tpu as pltpu
from jax.sharding import PartitionSpec as P

H = 16
K = 2
P_SIZE = 8
R1 = 16
R2 = 8
R3 = 256
LANES = 128
QT = 8
SCOPED = 2 * 2**20
SCOPED_UPDATE = 12 * 2**20


def generic_body(clique_a, message_in, clique_b, old_separator):
    p_local = clique_a.shape[1]
    q_total = clique_a.shape[3]
    r_total = clique_a.shape[4]
    absorbed = clique_a * message_in[:, None, :, None, :]
    column_width = r_total // R1
    summed = jnp.sum(absorbed, axis=(0, 2)) * (1.0 / (H * K))
    summed = summed.reshape(
        p_local, q_total, lax.axis_size("va") * (R1 // lax.axis_size("va")), column_width
    )
    shares = lax.psum_scatter(
        jnp.transpose(summed, (2, 0, 1, 3)), "va", scatter_dimension=0, tiled=True
    )
    shares = shares.reshape(shares.shape[0], p_local, q_total, R2, R3)
    moved = lax.all_to_all(shares, "vb", split_axis=3, concat_axis=1, tiled=True)
    separator = jnp.transpose(moved, (1, 2, 0, 3, 4))
    scaling = separator / old_separator
    updated_b = clique_b * scaling[None]
    partial_value = jnp.sum(updated_b, axis=(1, 4)) * (1.0 / (P_SIZE * R2))
    onward = lax.psum_scatter(partial_value, "vb", scatter_dimension=0, tiled=True)
    return (absorbed, updated_b, onward)


def tie(x, *after):
    return lax.optimization_barrier((x, *after))[0]


def in_hbm(x):
    return pltpu.with_memory_space_constraint(x, pltpu.HBM)


def swap(x, axis, mask):
    n = lax.axis_size(axis)
    return lax.ppermute(x, axis, [(i, i ^ mask) for i in range(n)])


def absorb_kernel(chunk, part, me_ref, z_ref, a_hbm, m_hbm, prod, s_ref, msg, sems, msems):
    n, nh, npl, nk, _, block = prod.shape
    nm, nr1, width = s_ref.shape[2], s_ref.shape[3], s_ref.shape[5]
    copies = []
    for g in range(n):
        lanes = pl.ds(pl.multiple_of((me_ref[0] ^ (2 * g + part)) * block, block), block)
        group = [pltpu.make_async_copy(m_hbm.at[:, :, lanes], msg.at[g], msems.at[g])]
        for h in range(nh):
            group.append(
                pltpu.make_async_copy(
                    a_hbm.at[h, :, :, pl.ds(chunk * QT, QT), lanes],
                    prod.at[g, h],
                    sems.at[g * nh + h],
                )
            )
        for copy in group:
            copy.start()
        copies.append(group)
    for g in range(n):
        for copy in copies[g]:
            copy.wait()
        for r1 in range(nr1):
            for m in range(nm):
                off = r1 * (nm * width) + (z_ref[0] ^ m) * width
                lanes = pl.ds(pl.multiple_of(off, width), width)
                rows = [
                    [
                        jnp.broadcast_to(msg[g, h, pl.ds(k, 1), lanes], (QT, width))
                        for k in range(nk)
                    ]
                    for h in range(nh)
                ]
                for p in range(npl):
                    total = None
                    for h in range(nh):
                        for k in range(nk):
                            value = prod[g, h, p, k, :, lanes] * rows[h][k]
                            prod[g, h, p, k, :, lanes] = value
                            total = value if total is None else total + value
                    s_ref[g, p, m, r1] = total


def absorb(me, z, clique_a, message, chunk, part, n_va, n_vb):
    nh, npl, nk, nq, nr = clique_a.shape
    block = nr // n_va
    nr1 = R1 // n_va
    width = block // nr1 // n_vb
    n = n_va // 2
    n_a = n * nh * npl * nk * QT * block
    return pl.pallas_call(
        functools.partial(absorb_kernel, chunk, part),
        in_specs=[
            pl.BlockSpec(memory_space=pltpu.SMEM),
            pl.BlockSpec(memory_space=pltpu.SMEM),
            pl.BlockSpec(memory_space=pltpu.HBM),
            pl.BlockSpec(memory_space=pltpu.HBM),
        ],
        out_specs=[pl.BlockSpec(memory_space=pltpu.VMEM)] * 2,
        out_shape=[
            pltpu.VMEM((n, nh, npl, nk, QT, block), clique_a.dtype),
            pltpu.VMEM((n, npl, n_vb, nr1, QT, width), clique_a.dtype),
        ],
        scratch_shapes=[
            pltpu.VMEM((n, nh, nk, block), jnp.float32),
            pltpu.SemaphoreType.DMA((n * nh,)),
            pltpu.SemaphoreType.DMA((n,)),
        ],
        compiler_params=pltpu.CompilerParams(vmem_limit_bytes=SCOPED),
        cost_estimate=pl.CostEstimate(flops=2 * n_a, bytes_accessed=4 * n_a, transcendentals=0),
        name="absorb",
    )(me, z, in_hbm(clique_a), in_hbm(message))


def flush_kernel(me_ref, *rest):
    prods, out, sems = rest[:-2], rest[-2], rest[-1]
    copies = []
    for i, prod in enumerate(prods):
        n, nh, block = prod.shape[0], prod.shape[1], prod.shape[5]
        chunk, part = i // 2, 1 - i % 2
        for g in range(n):
            lanes = pl.ds(pl.multiple_of((me_ref[0] ^ (2 * g + part)) * block, block), block)
            copies.append(
                pltpu.make_async_copy(
                    prod.at[g],
                    out.at[:, :, :, pl.ds(chunk * QT, QT), lanes],
                    sems.at[i * n + g],
                )
            )
    for copy in copies:
        copy.start()
    for copy in copies:
        copy.wait()


def flush(me, prods, like):
    return pl.pallas_call(
        flush_kernel,
        in_specs=[pl.BlockSpec(memory_space=pltpu.SMEM)]
        + [pl.BlockSpec(memory_space=pltpu.VMEM)] * len(prods),
        out_specs=pl.BlockSpec(memory_space=pltpu.HBM),
        out_shape=jax.ShapeDtypeStruct(like.shape, like.dtype),
        scratch_shapes=[pltpu.SemaphoreType.DMA((len(prods) * prods[0].shape[0],))],
        compiler_params=pltpu.CompilerParams(vmem_limit_bytes=SCOPED),
        cost_estimate=pl.CostEstimate(flops=0, bytes_accessed=4 * like.size, transcendentals=0),
        name="flush",
    )(me, *prods)


def fetch_kernel(orders, z_ref, b_hbm, *rest):
    helds, sems = rest[:-1], rest[-1]
    copies = []
    for order, held in zip(orders, helds):
        be = held.shape[1]
        for i, (m, half) in enumerate(order):
            part = b_hbm.at[pl.ds(((z_ref[0] ^ m) * 2 + half) * be, be)]
            copies.append(pltpu.make_async_copy(part, held.at[i], sems.at[len(copies)]))
    for copy in copies:
        copy.start()
    for copy in copies:
        copy.wait()


def fetch(z, b_rows, orders, n_vb):
    be = b_rows.shape[0] // n_vb // 2
    return pl.pallas_call(
        functools.partial(fetch_kernel, orders),
        in_specs=[
            pl.BlockSpec(memory_space=pltpu.SMEM),
            pl.BlockSpec(memory_space=pltpu.HBM),
        ],
        out_specs=[pl.BlockSpec(memory_space=pltpu.VMEM)] * len(orders),
        out_shape=[pltpu.VMEM((len(o), be) + b_rows.shape[1:], b_rows.dtype) for o in orders],
        scratch_shapes=[pltpu.SemaphoreType.DMA((sum(len(o) for o in orders),))],
        compiler_params=pltpu.CompilerParams(vmem_limit_bytes=SCOPED),
        cost_estimate=pl.CostEstimate(flops=0, bytes_accessed=4 * b_rows.size, transcendentals=0),
        name="fetch",
    )(z, in_hbm(b_rows))


def fill_scale(z_ref, old_ref, seps, scale):
    nc, npl, nr1, _, width = seps[0].shape
    nhi = R3 // LANES
    nr2 = width // R3
    tile = nr1 * nhi * nr2
    for m, sep in enumerate(seps):
        for p in range(npl):
            row = (z_ref[0] ^ m) * npl + p
            for c in range(nc):
                for r1 in range(nr1):
                    for r2 in range(nr2):
                        for hi in range(nhi):
                            at = (r2 * nhi + hi) * LANES
                            first = c * QT * tile + (r1 * nhi + hi) * nr2 + r2
                            scale[row, pl.ds(first, QT, stride=tile), :] = sep[
                                c, p, r1, :, at : at + LANES
                            ]
    for p in range(scale.shape[0]):
        scale[p] = scale[p] * (1.0 / (H * K)) / old_ref[p]


def update_kernel(order, dims, z_ref, held, scale, out, on_ref, stage, col, sems):
    nr1, nhi, nr2 = dims
    n, be, npt, rows, _ = held.shape
    tile = nr1 * nhi * nr2
    copies = []
    for i, (m, half) in enumerate(order):

        def one(e, carry, i=i):
            total = None
            for p in range(npt):
                value = held[i, e, p] * scale[p]
                stage[i, e, p] = value
                total = value if total is None else total + value
            col[...] = total * (1.0 / (P_SIZE * R2))
            for hi in range(nhi):
                for r1 in range(nr1):
                    acc = None
                    for r2 in range(nr2):
                        first = (r1 * nhi + hi) * nr2 + r2
                        piece = col[pl.ds(first, rows // tile, stride=tile), :]
                        acc = piece if acc is None else acc + piece
                    on_ref[i, e, pl.ds(hi * nr1 + r1, rows // tile, stride=nhi * nr1), :] = acc
            return carry

        lax.fori_loop(0, be, one, 0)
        copies.append(
            pltpu.make_async_copy(
                stage.at[i], out.at[pl.ds(((z_ref[0] ^ m) * 2 + half) * be, be)], sems.at[i]
            )
        )
        copies[-1].start()
    for copy in copies:
        copy.wait()


def first_update_kernel(order, dims, n_seps, z_ref, held, old_ref, *rest):
    seps, (out, on_ref, scale, stage, col, sems) = rest[:n_seps], rest[n_seps:]
    fill_scale(z_ref, old_ref, seps, scale)
    update_kernel(order, dims, z_ref, held, scale, out, on_ref, stage, col, sems)


def last_update_kernel(order, dims, z_ref, held, scale, before, out, on_ref, stage, col, sems):
    update_kernel(order, dims, z_ref, held, scale, out, on_ref, stage, col, sems)


def update(z, held, like, order, dims, seps=None, old=None, scale=None, before=None):
    n, be, npt, rows, lanes = held.shape
    nr1, nhi, nr2 = dims
    vmem = pl.BlockSpec(memory_space=pltpu.VMEM)
    hbm = pl.BlockSpec(memory_space=pltpu.HBM)
    out_specs = [hbm, vmem]
    out_shape = [
        jax.ShapeDtypeStruct(like.shape, like.dtype),
        pltpu.VMEM((n, be, rows // nr2, lanes), like.dtype),
    ]
    if before is None:
        kernel = functools.partial(first_update_kernel, order, dims, len(seps))
        args, in_specs, aliases = [z, held, old, *seps], [vmem] * (2 + len(seps)), {}
        out_specs.append(vmem)
        out_shape.append(pltpu.VMEM((npt, rows, lanes), like.dtype))
    else:
        kernel = functools.partial(last_update_kernel, order, dims)
        args, in_specs, aliases = [z, held, scale, before], [vmem, vmem, hbm], {3: 0}
    return pl.pallas_call(
        kernel,
        in_specs=[pl.BlockSpec(memory_space=pltpu.SMEM)] + in_specs,
        out_specs=out_specs,
        out_shape=out_shape,
        scratch_shapes=[
            pltpu.VMEM(held.shape, jnp.float32),
            pltpu.VMEM((rows, lanes), jnp.float32),
            pltpu.SemaphoreType.DMA((n,)),
        ],
        input_output_aliases=aliases,
        compiler_params=pltpu.CompilerParams(vmem_limit_bytes=SCOPED_UPDATE),
        cost_estimate=pl.CostEstimate(
            flops=2 * held.size, bytes_accessed=4 * held.size, transcendentals=0
        ),
        name="update",
    )(*args)


def body(clique_a, message_in, clique_b, old_separator):
    n_va, n_vb = lax.axis_size("va"), lax.axis_size("vb")
    nq = clique_a.shape[3]
    ne, npt, _, nr1, nr2, _ = clique_b.shape
    nhi = R3 // LANES
    n_chunks = nq // QT

    me = lax.axis_index("va").astype(jnp.int32).reshape(1)
    z = lax.axis_index("vb").astype(jnp.int32).reshape(1)

    def rows_view(x):
        lead = x.shape[:-3]
        x = x.reshape(lead + (nr1, nr2, nhi, LANES))
        n = len(lead)
        x = jnp.swapaxes(x, n + 1, n + 2)
        return x.reshape(lead[:-1] + (lead[-1] * nr1 * nhi * nr2, LANES))

    b_rows, old_rows = rows_view(clique_b), rows_view(old_separator)

    prods, first = [], []
    for c in range(n_chunks):
        prod, send = absorb(me, z, clique_a, message_in, c, 1, n_va, n_vb)
        prods.append(prod)
        got = swap(send, "va", 1)
        prod, keep = absorb(me, z, clique_a, message_in, c, 0, n_va, n_vb)
        prods.append(prod)
        keep = keep.reshape((2, 2) + keep.shape[1:])
        got = got.reshape(keep.shape)
        x0 = keep[:, 1, 0] + got[:, 1, 0]
        y1 = keep[1, :, 1] + got[1, :, 1]
        first.append((keep, got, swap(x0, "va", 2), swap(y1, "va", 4)))
    absorbed = flush(tie(me, x0, y1), prods, clique_a)

    pieces = [[] for _ in range(n_vb)]
    for keep, got, x0, y1 in first:
        y0 = keep[1, 0, 0] + got[1, 0, 0] + x0[1]
        x1 = keep[0, 1, 1] + got[0, 1, 1] + y1[1]
        k0 = keep[0, 0, 0] + got[0, 0, 0] + x0[0]
        k1 = keep[0, 0, 1] + got[0, 0, 1] + y1[0]
        y0_in, x1_in = swap(y0, "va", 4), swap(x1, "va", 2)
        for m in range(n_vb):
            pieces[m].append(jnp.stack([k0[m] + y0_in[m], k1[m] + x1_in[m]]))
    pieces = [jnp.stack(piece) for piece in pieces]
    seps = [pieces[0]] + [swap(pieces[m], "vb", m) for m in range(1, n_vb)]

    send_order = [(1, 0), (2, 0), (3, 1), (2, 1)]
    keep_order = [(0, 0), (3, 0), (0, 1), (1, 1)]
    dims = (nr1, nhi, nr2)
    held_s, held_k = fetch(tie(z, absorbed, y0, x1), b_rows, (send_order, keep_order), n_vb)
    updated, send, scale = update(z, held_s, b_rows, send_order, dims, seps=seps, old=old_rows)
    g0, g1 = swap(send[:2], "vb", 1), swap(send[2:], "vb", 3)
    updated, keep = update(z, held_k, b_rows, keep_order, dims, scale=scale, before=updated)
    s0, s1 = keep[1] + g0[1], keep[3] + g1[1]
    k0, k1 = keep[0] + g0[0], keep[2] + g1[0]
    s0, s1 = swap(s0, "vb", 3), swap(s1, "vb", 1)
    onward = jnp.concatenate([k0 + s0, k1 + s1], axis=0)

    e_out = ne // n_vb
    onward = onward.reshape(e_out, nq, nhi, nr1, LANES)
    onward = jnp.swapaxes(onward, 2, 3).reshape(e_out, nq, nr1, R3)
    updated = updated.reshape(ne, npt, nq, nr1, nhi, nr2, LANES)
    updated = jnp.swapaxes(updated, 4, 5).reshape(clique_b.shape)
    return (absorbed, updated, onward)


def solution(mesh):
    small = mesh.shape["va"] == 8 and mesh.shape["vb"] == 4
    return jax.shard_map(
        body if small else generic_body,
        mesh=mesh,
        in_specs=(
            P("va", "vb", None, None, None),
            P("va", None, None),
            P(None, None, None, "va", "vb", None),
            P(None, None, "va", "vb", None),
        ),
        out_specs=(
            P("va", "vb", None, None, None),
            P(None, None, None, "va", "vb", None),
            P("vb", None, "va", None),
        ),
        check_vma=False,
    )
```

```python
import functools

import jax
import jax.numpy as jnp
from jax import lax
from jax.experimental import pallas as pl
from jax.experimental.pallas import tpu as pltpu
from jax.sharding import PartitionSpec as P

H = 16
K = 2
P_SIZE = 8
R1 = 16
R2 = 8
R3 = 256
LANES = 128
QT = 8
SCOPED = 2 * 2**20
SCOPED_UPDATE = 12 * 2**20


def generic_body(clique_a, message_in, clique_b, old_separator):
    p_local = clique_a.shape[1]
    q_total = clique_a.shape[3]
    r_total = clique_a.shape[4]
    absorbed = clique_a * message_in[:, None, :, None, :]
    column_width = r_total // R1
    summed = jnp.sum(absorbed, axis=(0, 2)) * (1.0 / (H * K))
    summed = summed.reshape(
        p_local, q_total, lax.axis_size("va") * (R1 // lax.axis_size("va")), column_width
    )
    shares = lax.psum_scatter(
        jnp.transpose(summed, (2, 0, 1, 3)), "va", scatter_dimension=0, tiled=True
    )
    shares = shares.reshape(shares.shape[0], p_local, q_total, R2, R3)
    moved = lax.all_to_all(shares, "vb", split_axis=3, concat_axis=1, tiled=True)
    separator = jnp.transpose(moved, (1, 2, 0, 3, 4))
    scaling = separator / old_separator
    updated_b = clique_b * scaling[None]
    partial_value = jnp.sum(updated_b, axis=(1, 4)) * (1.0 / (P_SIZE * R2))
    onward = lax.psum_scatter(partial_value, "vb", scatter_dimension=0, tiled=True)
    return (absorbed, updated_b, onward)


def tie(x, *after):
    return lax.optimization_barrier((x, *after))[0]


def in_hbm(x):
    return pltpu.with_memory_space_constraint(x, pltpu.HBM)


def swap(x, axis, mask):
    n = lax.axis_size(axis)
    return lax.ppermute(x, axis, [(i, i ^ mask) for i in range(n)])


def absorb_kernel(chunk, part, me_ref, z_ref, a_hbm, m_hbm, prod, s_ref, msg, sems, msems):
    n, nh, npl, nk, _, block = prod.shape
    nm, nr1, width = s_ref.shape[2], s_ref.shape[3], s_ref.shape[5]
    copies = []
    for g in range(n):
        lanes = pl.ds(pl.multiple_of((me_ref[0] ^ (2 * g + part)) * block, block), block)
        group = [pltpu.make_async_copy(m_hbm.at[:, :, lanes], msg.at[g], msems.at[g])]
        for h in range(nh):
            group.append(
                pltpu.make_async_copy(
                    a_hbm.at[h, :, :, pl.ds(chunk * QT, QT), lanes],
                    prod.at[g, h],
                    sems.at[g * nh + h],
                )
            )
        for copy in group:
            copy.start()
        copies.append(group)
    for g in range(n):
        for copy in copies[g]:
            copy.wait()
        for r1 in range(nr1):
            for m in range(nm):
                off = r1 * (nm * width) + (z_ref[0] ^ m) * width
                lanes = pl.ds(pl.multiple_of(off, width), width)
                rows = [
                    [
                        jnp.broadcast_to(msg[g, h, pl.ds(k, 1), lanes], (QT, width))
                        for k in range(nk)
                    ]
                    for h in range(nh)
                ]
                for p in range(npl):
                    total = None
                    for h in range(nh):
                        for k in range(nk):
                            value = prod[g, h, p, k, :, lanes] * rows[h][k]
                            prod[g, h, p, k, :, lanes] = value
                            total = value if total is None else total + value
                    s_ref[g, p, m, r1] = total


def absorb(me, z, clique_a, message, chunk, part, n_va, n_vb):
    nh, npl, nk, nq, nr = clique_a.shape
    block = nr // n_va
    nr1 = R1 // n_va
    width = block // nr1 // n_vb
    n = n_va // 2
    n_a = n * nh * npl * nk * QT * block
    return pl.pallas_call(
        functools.partial(absorb_kernel, chunk, part),
        in_specs=[
            pl.BlockSpec(memory_space=pltpu.SMEM),
            pl.BlockSpec(memory_space=pltpu.SMEM),
            pl.BlockSpec(memory_space=pltpu.HBM),
            pl.BlockSpec(memory_space=pltpu.HBM),
        ],
        out_specs=[pl.BlockSpec(memory_space=pltpu.VMEM)] * 2,
        out_shape=[
            pltpu.VMEM((n, nh, npl, nk, QT, block), clique_a.dtype),
            pltpu.VMEM((n, npl, n_vb, nr1, QT, width), clique_a.dtype),
        ],
        scratch_shapes=[
            pltpu.VMEM((n, nh, nk, block), jnp.float32),
            pltpu.SemaphoreType.DMA((n * nh,)),
            pltpu.SemaphoreType.DMA((n,)),
        ],
        compiler_params=pltpu.CompilerParams(vmem_limit_bytes=SCOPED),
        cost_estimate=pl.CostEstimate(flops=2 * n_a, bytes_accessed=4 * n_a, transcendentals=0),
        name="absorb",
    )(me, z, in_hbm(clique_a), in_hbm(message))


def flush_kernel(me_ref, *rest):
    prods, out, sems = rest[:-2], rest[-2], rest[-1]
    copies = []
    for i, prod in enumerate(prods):
        n, nh, block = prod.shape[0], prod.shape[1], prod.shape[5]
        chunk, part = i // 2, 1 - i % 2
        for g in range(n):
            lanes = pl.ds(pl.multiple_of((me_ref[0] ^ (2 * g + part)) * block, block), block)
            copies.append(
                pltpu.make_async_copy(
                    prod.at[g],
                    out.at[:, :, :, pl.ds(chunk * QT, QT), lanes],
                    sems.at[i * n + g],
                )
            )
    for copy in copies:
        copy.start()
    for copy in copies:
        copy.wait()


def flush(me, prods, like):
    return pl.pallas_call(
        flush_kernel,
        in_specs=[pl.BlockSpec(memory_space=pltpu.SMEM)]
        + [pl.BlockSpec(memory_space=pltpu.VMEM)] * len(prods),
        out_specs=pl.BlockSpec(memory_space=pltpu.HBM),
        out_shape=jax.ShapeDtypeStruct(like.shape, like.dtype),
        scratch_shapes=[pltpu.SemaphoreType.DMA((len(prods) * prods[0].shape[0],))],
        compiler_params=pltpu.CompilerParams(vmem_limit_bytes=SCOPED),
        cost_estimate=pl.CostEstimate(flops=0, bytes_accessed=4 * like.size, transcendentals=0),
        name="flush",
    )(me, *prods)


def fetch_kernel(orders, z_ref, b_hbm, *rest):
    helds, sems = rest[:-1], rest[-1]
    copies = []
    for order, held in zip(orders, helds):
        be = held.shape[1]
        for i, (m, half) in enumerate(order):
            part = b_hbm.at[pl.ds(((z_ref[0] ^ m) * 2 + half) * be, be)]
            copies.append(pltpu.make_async_copy(part, held.at[i], sems.at[len(copies)]))
    for copy in copies:
        copy.start()
    for copy in copies:
        copy.wait()


def fetch(z, b_rows, orders, n_vb):
    be = b_rows.shape[0] // n_vb // 2
    return pl.pallas_call(
        functools.partial(fetch_kernel, orders),
        in_specs=[
            pl.BlockSpec(memory_space=pltpu.SMEM),
            pl.BlockSpec(memory_space=pltpu.HBM),
        ],
        out_specs=[pl.BlockSpec(memory_space=pltpu.VMEM)] * len(orders),
        out_shape=[pltpu.VMEM((len(o), be) + b_rows.shape[1:], b_rows.dtype) for o in orders],
        scratch_shapes=[pltpu.SemaphoreType.DMA((sum(len(o) for o in orders),))],
        compiler_params=pltpu.CompilerParams(vmem_limit_bytes=SCOPED),
        cost_estimate=pl.CostEstimate(flops=0, bytes_accessed=4 * b_rows.size, transcendentals=0),
        name="fetch",
    )(z, in_hbm(b_rows))


def fill_scale(z_ref, old_ref, seps, scale):
    nc, npl, nr1, _, width = seps[0].shape
    nhi = R3 // LANES
    nr2 = width // R3
    tile = nr1 * nhi * nr2
    for m, sep in enumerate(seps):
        for p in range(npl):
            row = (z_ref[0] ^ m) * npl + p
            for c in range(nc):
                for r1 in range(nr1):
                    for r2 in range(nr2):
                        for hi in range(nhi):
                            at = (r2 * nhi + hi) * LANES
                            first = c * QT * tile + (r1 * nhi + hi) * nr2 + r2
                            scale[row, pl.ds(first, QT, stride=tile), :] = sep[
                                c, p, r1, :, at : at + LANES
                            ]
    for p in range(scale.shape[0]):
        scale[p] = scale[p] * (1.0 / (H * K)) / old_ref[p]


def update_kernel(order, dims, z_ref, held, scale, out, on_ref, stage, col, sems):
    nr1, nhi, nr2 = dims
    n, be, npt, rows, _ = held.shape
    tile = nr1 * nhi * nr2
    copies = []
    for i, (m, half) in enumerate(order):

        def one(e, carry, i=i):
            total = None
            for p in range(npt):
                value = held[i, e, p] * scale[p]
                stage[i, e, p] = value
                total = value if total is None else total + value
            col[...] = total * (1.0 / (P_SIZE * R2))
            for hi in range(nhi):
                for r1 in range(nr1):
                    acc = None
                    for r2 in range(nr2):
                        first = (r1 * nhi + hi) * nr2 + r2
                        piece = col[pl.ds(first, rows // tile, stride=tile), :]
                        acc = piece if acc is None else acc + piece
                    on_ref[i, e, pl.ds(hi * nr1 + r1, rows // tile, stride=nhi * nr1), :] = acc
            return carry

        lax.fori_loop(0, be, one, 0)
        copies.append(
            pltpu.make_async_copy(
                stage.at[i], out.at[pl.ds(((z_ref[0] ^ m) * 2 + half) * be, be)], sems.at[i]
            )
        )
        copies[-1].start()
    for copy in copies:
        copy.wait()


def first_update_kernel(order, dims, n_seps, z_ref, held, old_ref, *rest):
    seps, (out, on_ref, scale, stage, col, sems) = rest[:n_seps], rest[n_seps:]
    fill_scale(z_ref, old_ref, seps, scale)
    update_kernel(order, dims, z_ref, held, scale, out, on_ref, stage, col, sems)


def last_update_kernel(order, dims, z_ref, held, scale, before, out, on_ref, stage, col, sems):
    update_kernel(order, dims, z_ref, held, scale, out, on_ref, stage, col, sems)


def update(z, held, like, order, dims, seps=None, old=None, scale=None, before=None):
    n, be, npt, rows, lanes = held.shape
    nr1, nhi, nr2 = dims
    vmem = pl.BlockSpec(memory_space=pltpu.VMEM)
    hbm = pl.BlockSpec(memory_space=pltpu.HBM)
    out_specs = [hbm, vmem]
    out_shape = [
        jax.ShapeDtypeStruct(like.shape, like.dtype),
        pltpu.VMEM((n, be, rows // nr2, lanes), like.dtype),
    ]
    if before is None:
        kernel = functools.partial(first_update_kernel, order, dims, len(seps))
        args, in_specs, aliases = [z, held, old, *seps], [vmem] * (2 + len(seps)), {}
        out_specs.append(vmem)
        out_shape.append(pltpu.VMEM((npt, rows, lanes), like.dtype))
    else:
        kernel = functools.partial(last_update_kernel, order, dims)
        args, in_specs, aliases = [z, held, scale, before], [vmem, vmem, hbm], {3: 0}
    return pl.pallas_call(
        kernel,
        in_specs=[pl.BlockSpec(memory_space=pltpu.SMEM)] + in_specs,
        out_specs=out_specs,
        out_shape=out_shape,
        scratch_shapes=[
            pltpu.VMEM(held.shape, jnp.float32),
            pltpu.VMEM((rows, lanes), jnp.float32),
            pltpu.SemaphoreType.DMA((n,)),
        ],
        input_output_aliases=aliases,
        compiler_params=pltpu.CompilerParams(vmem_limit_bytes=SCOPED_UPDATE),
        cost_estimate=pl.CostEstimate(
            flops=2 * held.size, bytes_accessed=4 * held.size, transcendentals=0
        ),
        name="update",
    )(*args)


def body(clique_a, message_in, clique_b, old_separator):
    n_va, n_vb = lax.axis_size("va"), lax.axis_size("vb")
    nq = clique_a.shape[3]
    ne, npt, _, nr1, nr2, _ = clique_b.shape
    nhi = R3 // LANES
    n_chunks = nq // QT

    me = lax.axis_index("va").astype(jnp.int32).reshape(1)
    z = lax.axis_index("vb").astype(jnp.int32).reshape(1)

    def rows_view(x):
        lead = x.shape[:-3]
        x = x.reshape(lead + (nr1, nr2, nhi, LANES))
        n = len(lead)
        x = jnp.swapaxes(x, n + 1, n + 2)
        return x.reshape(lead[:-1] + (lead[-1] * nr1 * nhi * nr2, LANES))

    b_rows, old_rows = rows_view(clique_b), rows_view(old_separator)

    prods, first, ready = [], [], me
    for c in range(n_chunks):
        prod, send = absorb(ready, z, clique_a, message_in, c, 1, n_va, n_vb)
        prods.append(prod)
        got = swap(send, "va", 1)
        prod, keep = absorb(tie(ready, send), z, clique_a, message_in, c, 0, n_va, n_vb)
        prods.append(prod)
        keep = keep.reshape((2, 2) + keep.shape[1:])
        got = got.reshape(keep.shape)
        x0 = keep[:, 1, 0] + got[:, 1, 0]
        y1 = keep[1, :, 1] + got[1, :, 1]
        ready = tie(me, x0, y1)
        first.append((keep, got, swap(x0, "va", 2), swap(y1, "va", 4)))

    absorbed = flush(ready, prods, clique_a)

    pieces = [[] for _ in range(n_vb)]
    for keep, got, x0, y1 in first:
        x0, y1 = tie(x0, ready), tie(y1, ready)
        y0 = keep[1, 0, 0] + got[1, 0, 0] + x0[1]
        x1 = keep[0, 1, 1] + got[0, 1, 1] + y1[1]
        k0 = keep[0, 0, 0] + got[0, 0, 0] + x0[0]
        k1 = keep[0, 0, 1] + got[0, 0, 1] + y1[0]
        y0_in, x1_in = swap(y0, "va", 4), swap(x1, "va", 2)
        for m in range(n_vb):
            pieces[m].append(jnp.stack([k0[m] + y0_in[m], k1[m] + x1_in[m]]))
    pieces = [jnp.stack(piece) for piece in pieces]
    seps = [pieces[0]] + [swap(pieces[m], "vb", m) for m in range(1, n_vb)]

    through, direct = [(2, 0), (2, 1)], [(1, 0), (3, 1)]
    forward, own = [(3, 0), (1, 1)], [(0, 0), (0, 1)]
    dims = (nr1, nhi, nr2)
    held_t, held_d = fetch(tie(z, absorbed, y0, x1), b_rows, (through, direct), n_vb)
    held_f, held_o = fetch(tie(z, held_d, *pieces[1:]), b_rows, (forward, own), n_vb)
    updated, sent, scale = update(z, held_t, b_rows, through, dims, seps=seps, old=old_rows)
    t0, t1 = swap(sent[0], "vb", 1), swap(sent[1], "vb", 3)
    updated, sent = update(z, held_d, b_rows, direct, dims, scale=scale, before=updated)
    d0, d1 = swap(sent[0], "vb", 1), swap(sent[1], "vb", 3)
    updated, kept = update(z, held_f, b_rows, forward, dims, scale=scale, before=updated)
    s0, s1 = swap(kept[0] + t0, "vb", 3), swap(kept[1] + t1, "vb", 1)
    updated, kept = update(z, held_o, b_rows, own, dims, scale=scale, before=updated)
    onward = jnp.concatenate([kept[0] + d0 + s0, kept[1] + d1 + s1], axis=0)

    e_out = ne // n_vb
    onward = onward.reshape(e_out, nq, nhi, nr1, LANES)
    onward = jnp.swapaxes(onward, 2, 3).reshape(e_out, nq, nr1, R3)
    updated = updated.reshape(ne, npt, nq, nr1, nhi, nr2, LANES)
    updated = jnp.swapaxes(updated, 4, 5).reshape(clique_b.shape)
    return (absorbed, updated, onward)


def solution(mesh):
    small = mesh.shape["va"] == 8 and mesh.shape["vb"] == 4
    return jax.shard_map(
        body if small else generic_body,
        mesh=mesh,
        in_specs=(
            P("va", "vb", None, None, None),
            P("va", None, None),
            P(None, None, None, "va", "vb", None),
            P(None, None, "va", "vb", None),
        ),
        out_specs=(
            P("va", "vb", None, None, None),
            P(None, None, None, "va", "vb", None),
            P("vb", None, "va", None),
        ),
        check_vma=False,
    )
```

```python
import functools

import jax
import jax.numpy as jnp
from jax import lax
from jax.experimental import pallas as pl
from jax.experimental.pallas import tpu as pltpu
from jax.sharding import PartitionSpec as P

H = 16
K = 2
P_SIZE = 8
R1 = 16
R2 = 8
R3 = 256
LANES = 128
QT = 8
SCOPED = 2 * 2**20
SCOPED_UPDATE = 12 * 2**20


def generic_body(clique_a, message_in, clique_b, old_separator):
    p_local = clique_a.shape[1]
    q_total = clique_a.shape[3]
    r_total = clique_a.shape[4]
    absorbed = clique_a * message_in[:, None, :, None, :]
    column_width = r_total // R1
    summed = jnp.sum(absorbed, axis=(0, 2)) * (1.0 / (H * K))
    summed = summed.reshape(
        p_local, q_total, lax.axis_size("va") * (R1 // lax.axis_size("va")), column_width
    )
    shares = lax.psum_scatter(
        jnp.transpose(summed, (2, 0, 1, 3)), "va", scatter_dimension=0, tiled=True
    )
    shares = shares.reshape(shares.shape[0], p_local, q_total, R2, R3)
    moved = lax.all_to_all(shares, "vb", split_axis=3, concat_axis=1, tiled=True)
    separator = jnp.transpose(moved, (1, 2, 0, 3, 4))
    scaling = separator / old_separator
    updated_b = clique_b * scaling[None]
    partial_value = jnp.sum(updated_b, axis=(1, 4)) * (1.0 / (P_SIZE * R2))
    onward = lax.psum_scatter(partial_value, "vb", scatter_dimension=0, tiled=True)
    return (absorbed, updated_b, onward)


def tie(x, *after):
    return lax.optimization_barrier((x, *after))[0]


def in_hbm(x):
    return pltpu.with_memory_space_constraint(x, pltpu.HBM)


def swap(x, axis, mask):
    n = lax.axis_size(axis)
    return lax.ppermute(x, axis, [(i, i ^ mask) for i in range(n)])


def absorb_kernel(chunk, part, me_ref, z_ref, a_hbm, m_hbm, prod, s_ref, msg, sems, msems):
    n, nh, npl, nk, _, block = prod.shape
    nm, nr1, width = s_ref.shape[2], s_ref.shape[3], s_ref.shape[5]
    copies = []
    for g in range(n):
        lanes = pl.ds(pl.multiple_of((me_ref[0] ^ (2 * g + part)) * block, block), block)
        group = [pltpu.make_async_copy(m_hbm.at[:, :, lanes], msg.at[g], msems.at[g])]
        for h in range(nh):
            group.append(
                pltpu.make_async_copy(
                    a_hbm.at[h, :, :, pl.ds(chunk * QT, QT), lanes],
                    prod.at[g, h],
                    sems.at[g * nh + h],
                )
            )
        for copy in group:
            copy.start()
        copies.append(group)
    for g in range(n):
        for copy in copies[g]:
            copy.wait()
        for r1 in range(nr1):
            for m in range(nm):
                off = r1 * (nm * width) + (z_ref[0] ^ m) * width
                lanes = pl.ds(pl.multiple_of(off, width), width)
                rows = [
                    [
                        jnp.broadcast_to(msg[g, h, pl.ds(k, 1), lanes], (QT, width))
                        for k in range(nk)
                    ]
                    for h in range(nh)
                ]
                for p in range(npl):
                    total = None
                    for h in range(nh):
                        for k in range(nk):
                            value = prod[g, h, p, k, :, lanes] * rows[h][k]
                            prod[g, h, p, k, :, lanes] = value
                            total = value if total is None else total + value
                    s_ref[g, p, m, r1] = total


def absorb(me, z, clique_a, message, chunk, part, n_va, n_vb):
    nh, npl, nk, nq, nr = clique_a.shape
    block = nr // n_va
    nr1 = R1 // n_va
    width = block // nr1 // n_vb
    n = n_va // 2
    n_a = n * nh * npl * nk * QT * block
    return pl.pallas_call(
        functools.partial(absorb_kernel, chunk, part),
        in_specs=[
            pl.BlockSpec(memory_space=pltpu.SMEM),
            pl.BlockSpec(memory_space=pltpu.SMEM),
            pl.BlockSpec(memory_space=pltpu.HBM),
            pl.BlockSpec(memory_space=pltpu.HBM),
        ],
        out_specs=[pl.BlockSpec(memory_space=pltpu.VMEM)] * 2,
        out_shape=[
            pltpu.VMEM((n, nh, npl, nk, QT, block), clique_a.dtype),
            pltpu.VMEM((n, npl, n_vb, nr1, QT, width), clique_a.dtype),
        ],
        scratch_shapes=[
            pltpu.VMEM((n, nh, nk, block), jnp.float32),
            pltpu.SemaphoreType.DMA((n * nh,)),
            pltpu.SemaphoreType.DMA((n,)),
        ],
        compiler_params=pltpu.CompilerParams(vmem_limit_bytes=SCOPED),
        cost_estimate=pl.CostEstimate(flops=2 * n_a, bytes_accessed=4 * n_a, transcendentals=0),
        name="absorb",
    )(me, z, in_hbm(clique_a), in_hbm(message))


def flush_kernel(me_ref, *rest):
    prods, out, sems = rest[:-2], rest[-2], rest[-1]
    copies = []
    for i, prod in enumerate(prods):
        n, nh, block = prod.shape[0], prod.shape[1], prod.shape[5]
        chunk, part = i // 2, 1 - i % 2
        for g in range(n):
            lanes = pl.ds(pl.multiple_of((me_ref[0] ^ (2 * g + part)) * block, block), block)
            copies.append(
                pltpu.make_async_copy(
                    prod.at[g],
                    out.at[:, :, :, pl.ds(chunk * QT, QT), lanes],
                    sems.at[i * n + g],
                )
            )
    for copy in copies:
        copy.start()
    for copy in copies:
        copy.wait()


def flush(me, prods, like):
    return pl.pallas_call(
        flush_kernel,
        in_specs=[pl.BlockSpec(memory_space=pltpu.SMEM)]
        + [pl.BlockSpec(memory_space=pltpu.VMEM)] * len(prods),
        out_specs=pl.BlockSpec(memory_space=pltpu.HBM),
        out_shape=jax.ShapeDtypeStruct(like.shape, like.dtype),
        scratch_shapes=[pltpu.SemaphoreType.DMA((len(prods) * prods[0].shape[0],))],
        compiler_params=pltpu.CompilerParams(vmem_limit_bytes=SCOPED),
        cost_estimate=pl.CostEstimate(flops=0, bytes_accessed=4 * like.size, transcendentals=0),
        name="flush",
    )(me, *prods)


def fetch_kernel(orders, z_ref, b_hbm, *rest):
    helds, sems = rest[:-1], rest[-1]
    copies = []
    for order, held in zip(orders, helds):
        be = held.shape[1]
        for i, (m, half) in enumerate(order):
            part = b_hbm.at[pl.ds(((z_ref[0] ^ m) * 2 + half) * be, be)]
            copies.append(pltpu.make_async_copy(part, held.at[i], sems.at[len(copies)]))
    for copy in copies:
        copy.start()
    for copy in copies:
        copy.wait()


def fetch(z, b_rows, orders, n_vb):
    be = b_rows.shape[0] // n_vb // 2
    return pl.pallas_call(
        functools.partial(fetch_kernel, orders),
        in_specs=[
            pl.BlockSpec(memory_space=pltpu.SMEM),
            pl.BlockSpec(memory_space=pltpu.HBM),
        ],
        out_specs=[pl.BlockSpec(memory_space=pltpu.VMEM)] * len(orders),
        out_shape=[pltpu.VMEM((len(o), be) + b_rows.shape[1:], b_rows.dtype) for o in orders],
        scratch_shapes=[pltpu.SemaphoreType.DMA((sum(len(o) for o in orders),))],
        compiler_params=pltpu.CompilerParams(vmem_limit_bytes=SCOPED),
        cost_estimate=pl.CostEstimate(flops=0, bytes_accessed=4 * b_rows.size, transcendentals=0),
        name="fetch",
    )(z, in_hbm(b_rows))


def fill_scale(z_ref, old_ref, seps, scale):
    nc, npl, nr1, _, width = seps[0].shape
    nhi = R3 // LANES
    nr2 = width // R3
    tile = nr1 * nhi * nr2
    for m, sep in enumerate(seps):
        for p in range(npl):
            row = (z_ref[0] ^ m) * npl + p
            for c in range(nc):
                for r1 in range(nr1):
                    for r2 in range(nr2):
                        for hi in range(nhi):
                            at = (r2 * nhi + hi) * LANES
                            first = c * QT * tile + (r1 * nhi + hi) * nr2 + r2
                            scale[row, pl.ds(first, QT, stride=tile), :] = sep[
                                c, p, r1, :, at : at + LANES
                            ]
    for p in range(scale.shape[0]):
        scale[p] = scale[p] * (1.0 / (H * K)) / old_ref[p]


def update_kernel(order, dims, z_ref, held, scale, out, on_ref, stage, col, sems):
    nr1, nhi, nr2 = dims
    n, be, npt, rows, _ = held.shape
    tile = nr1 * nhi * nr2
    copies = []
    for i, (m, half) in enumerate(order):

        def one(e, carry, i=i):
            total = None
            for p in range(npt):
                value = held[i, e, p] * scale[p]
                stage[i, e, p] = value
                total = value if total is None else total + value
            col[...] = total * (1.0 / (P_SIZE * R2))
            for hi in range(nhi):
                for r1 in range(nr1):
                    acc = None
                    for r2 in range(nr2):
                        first = (r1 * nhi + hi) * nr2 + r2
                        piece = col[pl.ds(first, rows // tile, stride=tile), :]
                        acc = piece if acc is None else acc + piece
                    on_ref[i, e, pl.ds(hi * nr1 + r1, rows // tile, stride=nhi * nr1), :] = acc
            return carry

        lax.fori_loop(0, be, one, 0)
        copies.append(
            pltpu.make_async_copy(
                stage.at[i], out.at[pl.ds(((z_ref[0] ^ m) * 2 + half) * be, be)], sems.at[i]
            )
        )
        copies[-1].start()
    for copy in copies:
        copy.wait()


def first_update_kernel(order, dims, n_seps, z_ref, held, old_ref, *rest):
    seps, (out, on_ref, scale, stage, col, sems) = rest[:n_seps], rest[n_seps:]
    fill_scale(z_ref, old_ref, seps, scale)
    update_kernel(order, dims, z_ref, held, scale, out, on_ref, stage, col, sems)


def last_update_kernel(order, dims, z_ref, held, scale, before, out, on_ref, stage, col, sems):
    update_kernel(order, dims, z_ref, held, scale, out, on_ref, stage, col, sems)


def update(z, held, like, order, dims, seps=None, old=None, scale=None, before=None):
    n, be, npt, rows, lanes = held.shape
    nr1, nhi, nr2 = dims
    vmem = pl.BlockSpec(memory_space=pltpu.VMEM)
    hbm = pl.BlockSpec(memory_space=pltpu.HBM)
    out_specs = [hbm, vmem]
    out_shape = [
        jax.ShapeDtypeStruct(like.shape, like.dtype),
        pltpu.VMEM((n, be, rows // nr2, lanes), like.dtype),
    ]
    if before is None:
        kernel = functools.partial(first_update_kernel, order, dims, len(seps))
        args, in_specs, aliases = [z, held, old, *seps], [vmem] * (2 + len(seps)), {}
        out_specs.append(vmem)
        out_shape.append(pltpu.VMEM((npt, rows, lanes), like.dtype))
    else:
        kernel = functools.partial(last_update_kernel, order, dims)
        args, in_specs, aliases = [z, held, scale, before], [vmem, vmem, hbm], {3: 0}
    return pl.pallas_call(
        kernel,
        in_specs=[pl.BlockSpec(memory_space=pltpu.SMEM)] + in_specs,
        out_specs=out_specs,
        out_shape=out_shape,
        scratch_shapes=[
            pltpu.VMEM(held.shape, jnp.float32),
            pltpu.VMEM((rows, lanes), jnp.float32),
            pltpu.SemaphoreType.DMA((n,)),
        ],
        input_output_aliases=aliases,
        compiler_params=pltpu.CompilerParams(vmem_limit_bytes=SCOPED_UPDATE),
        cost_estimate=pl.CostEstimate(
            flops=2 * held.size, bytes_accessed=4 * held.size, transcendentals=0
        ),
        name="update",
    )(*args)


def body(clique_a, message_in, clique_b, old_separator):
    n_va, n_vb = lax.axis_size("va"), lax.axis_size("vb")
    nq = clique_a.shape[3]
    ne, npt, _, nr1, nr2, _ = clique_b.shape
    nhi = R3 // LANES
    n_chunks = nq // QT

    me = lax.axis_index("va").astype(jnp.int32).reshape(1)
    z = lax.axis_index("vb").astype(jnp.int32).reshape(1)

    def rows_view(x):
        lead = x.shape[:-3]
        x = x.reshape(lead + (nr1, nr2, nhi, LANES))
        n = len(lead)
        x = jnp.swapaxes(x, n + 1, n + 2)
        return x.reshape(lead[:-1] + (lead[-1] * nr1 * nhi * nr2, LANES))

    b_rows, old_rows = rows_view(clique_b), rows_view(old_separator)

    prods, first, ready = [], [], me
    for c in range(n_chunks):
        prod, send = absorb(ready, z, clique_a, message_in, c, 1, n_va, n_vb)
        prods.append(prod)
        got = swap(send, "va", 1)
        prod, keep = absorb(tie(ready, send), z, clique_a, message_in, c, 0, n_va, n_vb)
        prods.append(prod)
        keep = keep.reshape((2, 2) + keep.shape[1:])
        got = got.reshape(keep.shape)
        x0 = keep[:, 1, 0] + got[:, 1, 0]
        y1 = keep[1, :, 1] + got[1, :, 1]
        ready = tie(me, x0, y1)
        first.append((keep, got, swap(x0, "va", 2), swap(y1, "va", 4)))

    absorbed = flush(ready, prods, clique_a)

    pieces = [[] for _ in range(n_vb)]
    for keep, got, x0, y1 in first:
        x0, y1 = tie(x0, ready), tie(y1, ready)
        y0 = keep[1, 0, 0] + got[1, 0, 0] + x0[1]
        x1 = keep[0, 1, 1] + got[0, 1, 1] + y1[1]
        k0 = keep[0, 0, 0] + got[0, 0, 0] + x0[0]
        k1 = keep[0, 0, 1] + got[0, 0, 1] + y1[0]
        y0_in, x1_in = swap(y0, "va", 4), swap(x1, "va", 2)
        for m in range(n_vb):
            pieces[m].append(jnp.stack([k0[m] + y0_in[m], k1[m] + x1_in[m]]))
    far = n_vb // 2
    early = swap(pieces[far][0], "vb", far)
    late = swap(pieces[far][1], "vb", far)
    pieces = [jnp.stack(piece) for piece in pieces]
    seps = [pieces[0]] + [swap(pieces[m], "vb", m) if m != far else None for m in range(1, n_vb)]
    seps[far] = jnp.stack([early, late])

    through, middle = [(2, 0), (2, 1)], [(1, 0), (3, 1), (3, 0), (1, 1)]
    own = [(0, 0), (0, 1)]
    dims = (nr1, nhi, nr2)
    held_t, held_o = fetch(tie(z, absorbed, y0, x1), b_rows, (through, own), n_vb)
    (held_m,) = fetch(tie(z, held_o, *pieces[1:]), b_rows, (middle,), n_vb)
    updated, sent, scale = update(z, held_t, b_rows, through, dims, seps=seps, old=old_rows)
    t0, t1 = swap(sent[0], "vb", 1), swap(sent[1], "vb", 3)
    updated, sent = update(z, held_m, b_rows, middle, dims, scale=scale, before=updated)
    d0, d1 = swap(sent[0], "vb", 1), swap(sent[1], "vb", 3)
    s0, s1 = swap(sent[2] + t0, "vb", 3), swap(sent[3] + t1, "vb", 1)
    updated, kept = update(z, held_o, b_rows, own, dims, scale=scale, before=updated)
    onward = jnp.concatenate([kept[0] + d0 + s0, kept[1] + d1 + s1], axis=0)

    e_out = ne // n_vb
    onward = onward.reshape(e_out, nq, nhi, nr1, LANES)
    onward = jnp.swapaxes(onward, 2, 3).reshape(e_out, nq, nr1, R3)
    updated = updated.reshape(ne, npt, nq, nr1, nhi, nr2, LANES)
    updated = jnp.swapaxes(updated, 4, 5).reshape(clique_b.shape)
    return (absorbed, updated, onward)


def solution(mesh):
    small = mesh.shape["va"] == 8 and mesh.shape["vb"] == 4
    return jax.shard_map(
        body if small else generic_body,
        mesh=mesh,
        in_specs=(
            P("va", "vb", None, None, None),
            P("va", None, None),
            P(None, None, None, "va", "vb", None),
            P(None, None, "va", "vb", None),
        ),
        out_specs=(
            P("va", "vb", None, None, None),
            P(None, None, None, "va", "vb", None),
            P("vb", None, "va", None),
        ),
        check_vma=False,
    )
```

```python
import functools

import jax
import jax.numpy as jnp
from jax import lax
from jax.experimental import pallas as pl
from jax.experimental.pallas import tpu as pltpu
from jax.sharding import PartitionSpec as P

H = 16
K = 2
P_SIZE = 8
R1 = 16
R2 = 8
R3 = 256
LANES = 128
QT = 8
SCOPED = 2 * 2**20
SCOPED_UPDATE = 12 * 2**20


def generic_body(clique_a, message_in, clique_b, old_separator):
    p_local = clique_a.shape[1]
    q_total = clique_a.shape[3]
    r_total = clique_a.shape[4]
    absorbed = clique_a * message_in[:, None, :, None, :]
    column_width = r_total // R1
    summed = jnp.sum(absorbed, axis=(0, 2)) * (1.0 / (H * K))
    summed = summed.reshape(
        p_local, q_total, lax.axis_size("va") * (R1 // lax.axis_size("va")), column_width
    )
    shares = lax.psum_scatter(
        jnp.transpose(summed, (2, 0, 1, 3)), "va", scatter_dimension=0, tiled=True
    )
    shares = shares.reshape(shares.shape[0], p_local, q_total, R2, R3)
    moved = lax.all_to_all(shares, "vb", split_axis=3, concat_axis=1, tiled=True)
    separator = jnp.transpose(moved, (1, 2, 0, 3, 4))
    scaling = separator / old_separator
    updated_b = clique_b * scaling[None]
    partial_value = jnp.sum(updated_b, axis=(1, 4)) * (1.0 / (P_SIZE * R2))
    onward = lax.psum_scatter(partial_value, "vb", scatter_dimension=0, tiled=True)
    return (absorbed, updated_b, onward)


def tie(x, *after):
    return lax.optimization_barrier((x, *after))[0]


def in_hbm(x):
    return pltpu.with_memory_space_constraint(x, pltpu.HBM)


def swap(x, axis, mask):
    n = lax.axis_size(axis)
    return lax.ppermute(x, axis, [(i, i ^ mask) for i in range(n)])


def absorb_kernel(chunk, part, me_ref, z_ref, a_hbm, m_hbm, prod, s_ref, msg, sems, msems):
    n, nh, npl, nk, _, block = prod.shape
    nm, nr1, width = s_ref.shape[2], s_ref.shape[3], s_ref.shape[5]
    copies = []
    for g in range(n):
        lanes = pl.ds(pl.multiple_of((me_ref[0] ^ (2 * g + part)) * block, block), block)
        group = [pltpu.make_async_copy(m_hbm.at[:, :, lanes], msg.at[g], msems.at[g])]
        for h in range(nh):
            group.append(
                pltpu.make_async_copy(
                    a_hbm.at[h, :, :, pl.ds(chunk * QT, QT), lanes],
                    prod.at[g, h],
                    sems.at[g * nh + h],
                )
            )
        for copy in group:
            copy.start()
        copies.append(group)
    for g in range(n):
        for copy in copies[g]:
            copy.wait()
        for r1 in range(nr1):
            for m in range(nm):
                off = r1 * (nm * width) + (z_ref[0] ^ m) * width
                lanes = pl.ds(pl.multiple_of(off, width), width)
                rows = [
                    [
                        jnp.broadcast_to(msg[g, h, pl.ds(k, 1), lanes], (QT, width))
                        for k in range(nk)
                    ]
                    for h in range(nh)
                ]
                for p in range(npl):
                    total = None
                    for h in range(nh):
                        for k in range(nk):
                            value = prod[g, h, p, k, :, lanes] * rows[h][k]
                            prod[g, h, p, k, :, lanes] = value
                            total = value if total is None else total + value
                    s_ref[g, p, m, r1] = total


def absorb(me, z, clique_a, message, chunk, part, n_va, n_vb):
    nh, npl, nk, nq, nr = clique_a.shape
    block = nr // n_va
    nr1 = R1 // n_va
    width = block // nr1 // n_vb
    n = n_va // 2
    n_a = n * nh * npl * nk * QT * block
    return pl.pallas_call(
        functools.partial(absorb_kernel, chunk, part),
        in_specs=[
            pl.BlockSpec(memory_space=pltpu.SMEM),
            pl.BlockSpec(memory_space=pltpu.SMEM),
            pl.BlockSpec(memory_space=pltpu.HBM),
            pl.BlockSpec(memory_space=pltpu.HBM),
        ],
        out_specs=[pl.BlockSpec(memory_space=pltpu.VMEM)] * 2,
        out_shape=[
            pltpu.VMEM((n, nh, npl, nk, QT, block), clique_a.dtype),
            pltpu.VMEM((n, npl, n_vb, nr1, QT, width), clique_a.dtype),
        ],
        scratch_shapes=[
            pltpu.VMEM((n, nh, nk, block), jnp.float32),
            pltpu.SemaphoreType.DMA((n * nh,)),
            pltpu.SemaphoreType.DMA((n,)),
        ],
        compiler_params=pltpu.CompilerParams(vmem_limit_bytes=SCOPED),
        cost_estimate=pl.CostEstimate(flops=2 * n_a, bytes_accessed=4 * n_a, transcendentals=0),
        name="absorb",
    )(me, z, in_hbm(clique_a), in_hbm(message))


def flush_kernel(me_ref, *rest):
    prods, out, sems = rest[:-2], rest[-2], rest[-1]
    copies = []
    for i, prod in enumerate(prods):
        n, nh, block = prod.shape[0], prod.shape[1], prod.shape[5]
        chunk, part = i // 2, 1 - i % 2
        for g in range(n):
            lanes = pl.ds(pl.multiple_of((me_ref[0] ^ (2 * g + part)) * block, block), block)
            copies.append(
                pltpu.make_async_copy(
                    prod.at[g],
                    out.at[:, :, :, pl.ds(chunk * QT, QT), lanes],
                    sems.at[i * n + g],
                )
            )
    for copy in copies:
        copy.start()
    for copy in copies:
        copy.wait()


def flush(me, prods, like):
    return pl.pallas_call(
        flush_kernel,
        in_specs=[pl.BlockSpec(memory_space=pltpu.SMEM)]
        + [pl.BlockSpec(memory_space=pltpu.VMEM)] * len(prods),
        out_specs=pl.BlockSpec(memory_space=pltpu.HBM),
        out_shape=jax.ShapeDtypeStruct(like.shape, like.dtype),
        scratch_shapes=[pltpu.SemaphoreType.DMA((len(prods) * prods[0].shape[0],))],
        compiler_params=pltpu.CompilerParams(vmem_limit_bytes=SCOPED),
        cost_estimate=pl.CostEstimate(flops=0, bytes_accessed=4 * like.size, transcendentals=0),
        name="flush",
    )(me, *prods)


def fetch_kernel(orders, z_ref, b_hbm, *rest):
    helds, sems = rest[:-1], rest[-1]
    copies = []
    for order, held in zip(orders, helds):
        be = held.shape[1]
        for i, (m, half) in enumerate(order):
            part = b_hbm.at[pl.ds(((z_ref[0] ^ m) * 2 + half) * be, be)]
            copies.append(pltpu.make_async_copy(part, held.at[i], sems.at[len(copies)]))
    for copy in copies:
        copy.start()
    for copy in copies:
        copy.wait()


def fetch(z, b_rows, orders, n_vb):
    be = b_rows.shape[0] // n_vb // 2
    return pl.pallas_call(
        functools.partial(fetch_kernel, orders),
        in_specs=[
            pl.BlockSpec(memory_space=pltpu.SMEM),
            pl.BlockSpec(memory_space=pltpu.HBM),
        ],
        out_specs=[pl.BlockSpec(memory_space=pltpu.VMEM)] * len(orders),
        out_shape=[pltpu.VMEM((len(o), be) + b_rows.shape[1:], b_rows.dtype) for o in orders],
        scratch_shapes=[pltpu.SemaphoreType.DMA((sum(len(o) for o in orders),))],
        compiler_params=pltpu.CompilerParams(vmem_limit_bytes=SCOPED),
        cost_estimate=pl.CostEstimate(flops=0, bytes_accessed=4 * b_rows.size, transcendentals=0),
        name="fetch",
    )(z, in_hbm(b_rows))


def fill_scale(z_ref, old_ref, seps, scale):
    nc, npl, nr1, _, width = seps[0].shape
    nhi = R3 // LANES
    nr2 = width // R3
    tile = nr1 * nhi * nr2
    for m, sep in enumerate(seps):
        for p in range(npl):
            row = (z_ref[0] ^ m) * npl + p
            for c in range(nc):
                for r1 in range(nr1):
                    for r2 in range(nr2):
                        for hi in range(nhi):
                            at = (r2 * nhi + hi) * LANES
                            first = c * QT * tile + (r1 * nhi + hi) * nr2 + r2
                            scale[row, pl.ds(first, QT, stride=tile), :] = sep[
                                c, p, r1, :, at : at + LANES
                            ]
    for p in range(scale.shape[0]):
        scale[p] = scale[p] * (1.0 / (H * K)) / old_ref[p]


def update_kernel(order, dims, z_ref, held, scale, out, on_ref, stage, col, sems):
    nr1, nhi, nr2 = dims
    n, be, npt, rows, _ = held.shape
    tile = nr1 * nhi * nr2
    copies = []
    for i, (m, half) in enumerate(order):

        def one(e, carry, i=i):
            total = None
            for p in range(npt):
                value = held[i, e, p] * scale[p]
                stage[i, e, p] = value
                total = value if total is None else total + value
            col[...] = total * (1.0 / (P_SIZE * R2))
            for hi in range(nhi):
                for r1 in range(nr1):
                    acc = None
                    for r2 in range(nr2):
                        first = (r1 * nhi + hi) * nr2 + r2
                        piece = col[pl.ds(first, rows // tile, stride=tile), :]
                        acc = piece if acc is None else acc + piece
                    on_ref[i, e, pl.ds(hi * nr1 + r1, rows // tile, stride=nhi * nr1), :] = acc
            return carry

        lax.fori_loop(0, be, one, 0)
        copies.append(
            pltpu.make_async_copy(
                stage.at[i], out.at[pl.ds(((z_ref[0] ^ m) * 2 + half) * be, be)], sems.at[i]
            )
        )
        copies[-1].start()
    for copy in copies:
        copy.wait()


def first_update_kernel(order, dims, n_seps, z_ref, held, old_ref, *rest):
    seps, (out, on_ref, scale, stage, col, sems) = rest[:n_seps], rest[n_seps:]
    fill_scale(z_ref, old_ref, seps, scale)
    update_kernel(order, dims, z_ref, held, scale, out, on_ref, stage, col, sems)


def last_update_kernel(order, dims, z_ref, held, scale, before, out, on_ref, stage, col, sems):
    update_kernel(order, dims, z_ref, held, scale, out, on_ref, stage, col, sems)


def update(z, held, like, order, dims, seps=None, old=None, scale=None, before=None):
    n, be, npt, rows, lanes = held.shape
    nr1, nhi, nr2 = dims
    vmem = pl.BlockSpec(memory_space=pltpu.VMEM)
    hbm = pl.BlockSpec(memory_space=pltpu.HBM)
    out_specs = [hbm, vmem]
    out_shape = [
        jax.ShapeDtypeStruct(like.shape, like.dtype),
        pltpu.VMEM((n, be, rows // nr2, lanes), like.dtype),
    ]
    if before is None:
        kernel = functools.partial(first_update_kernel, order, dims, len(seps))
        args, in_specs, aliases = [z, held, old, *seps], [vmem] * (2 + len(seps)), {}
        out_specs.append(vmem)
        out_shape.append(pltpu.VMEM((npt, rows, lanes), like.dtype))
    else:
        kernel = functools.partial(last_update_kernel, order, dims)
        args, in_specs, aliases = [z, held, scale, before], [vmem, vmem, hbm], {3: 0}
    return pl.pallas_call(
        kernel,
        in_specs=[pl.BlockSpec(memory_space=pltpu.SMEM)] + in_specs,
        out_specs=out_specs,
        out_shape=out_shape,
        scratch_shapes=[
            pltpu.VMEM(held.shape, jnp.float32),
            pltpu.VMEM((rows, lanes), jnp.float32),
            pltpu.SemaphoreType.DMA((n,)),
        ],
        input_output_aliases=aliases,
        compiler_params=pltpu.CompilerParams(vmem_limit_bytes=SCOPED_UPDATE),
        cost_estimate=pl.CostEstimate(
            flops=2 * held.size, bytes_accessed=4 * held.size, transcendentals=0
        ),
        name="update",
    )(*args)


def body(clique_a, message_in, clique_b, old_separator):
    n_va, n_vb = lax.axis_size("va"), lax.axis_size("vb")
    nq = clique_a.shape[3]
    ne, npt, _, nr1, nr2, _ = clique_b.shape
    nhi = R3 // LANES
    n_chunks = nq // QT

    me = lax.axis_index("va").astype(jnp.int32).reshape(1)
    z = lax.axis_index("vb").astype(jnp.int32).reshape(1)

    def rows_view(x):
        lead = x.shape[:-3]
        x = x.reshape(lead + (nr1, nr2, nhi, LANES))
        n = len(lead)
        x = jnp.swapaxes(x, n + 1, n + 2)
        return x.reshape(lead[:-1] + (lead[-1] * nr1 * nhi * nr2, LANES))

    b_rows, old_rows = rows_view(clique_b), rows_view(old_separator)

    prods, first, ready = [], [], me
    for c in range(n_chunks):
        prod, send = absorb(ready, z, clique_a, message_in, c, 1, n_va, n_vb)
        prods.append(prod)
        got = swap(send, "va", 1)
        prod, keep = absorb(tie(ready, send), z, clique_a, message_in, c, 0, n_va, n_vb)
        prods.append(prod)
        keep = keep.reshape((2, 2) + keep.shape[1:])
        got = got.reshape(keep.shape)
        x0 = keep[:, 1, 0] + got[:, 1, 0]
        y1 = keep[1, :, 1] + got[1, :, 1]
        ready = tie(me, x0, y1)
        first.append((keep, got, swap(x0, "va", 2), swap(y1, "va", 4)))

    absorbed = flush(ready, prods, clique_a)

    pieces = [[] for _ in range(n_vb)]
    for keep, got, x0, y1 in first:
        x0, y1 = tie(x0, ready), tie(y1, ready)
        y0 = keep[1, 0, 0] + got[1, 0, 0] + x0[1]
        x1 = keep[0, 1, 1] + got[0, 1, 1] + y1[1]
        k0 = keep[0, 0, 0] + got[0, 0, 0] + x0[0]
        k1 = keep[0, 0, 1] + got[0, 0, 1] + y1[0]
        y0_in, x1_in = swap(y0, "va", 4), swap(x1, "va", 2)
        for m in range(n_vb):
            pieces[m].append(jnp.stack([k0[m] + y0_in[m], k1[m] + x1_in[m]]))
    far = n_vb // 2
    early = swap(tie(pieces[far][0], y0, x1), "vb", far)
    late = swap(pieces[far][1], "vb", far)
    pieces = [jnp.stack(piece) for piece in pieces]
    seps = [pieces[0]] + [swap(pieces[m], "vb", m) if m != far else None for m in range(1, n_vb)]
    seps[far] = jnp.stack([early, late])

    through, middle = [(2, 0), (2, 1)], [(1, 0), (3, 1), (3, 0), (1, 1)]
    own = [(0, 0), (0, 1)]
    dims = (nr1, nhi, nr2)
    held_t, held_o = fetch(tie(z, absorbed, y0, x1), b_rows, (through, own), n_vb)
    (held_m,) = fetch(tie(z, held_o, *pieces[1:]), b_rows, (middle,), n_vb)
    updated, sent, scale = update(z, held_t, b_rows, through, dims, seps=seps, old=old_rows)
    t0, t1 = swap(sent[0], "vb", 1), swap(sent[1], "vb", 3)
    updated, sent = update(z, held_m, b_rows, middle, dims, scale=scale, before=updated)
    d0, d1 = swap(sent[0], "vb", 1), swap(sent[1], "vb", 3)
    s0, s1 = swap(sent[2] + t0, "vb", 3), swap(sent[3] + t1, "vb", 1)
    updated, kept = update(z, held_o, b_rows, own, dims, scale=scale, before=updated)
    onward = jnp.concatenate([kept[0] + d0 + s0, kept[1] + d1 + s1], axis=0)

    e_out = ne // n_vb
    onward = onward.reshape(e_out, nq, nhi, nr1, LANES)
    onward = jnp.swapaxes(onward, 2, 3).reshape(e_out, nq, nr1, R3)
    updated = updated.reshape(ne, npt, nq, nr1, nhi, nr2, LANES)
    updated = jnp.swapaxes(updated, 4, 5).reshape(clique_b.shape)
    return (absorbed, updated, onward)


def solution(mesh):
    small = mesh.shape["va"] == 8 and mesh.shape["vb"] == 4
    return jax.shard_map(
        body if small else generic_body,
        mesh=mesh,
        in_specs=(
            P("va", "vb", None, None, None),
            P("va", None, None),
            P(None, None, None, "va", "vb", None),
            P(None, None, "va", "vb", None),
        ),
        out_specs=(
            P("va", "vb", None, None, None),
            P(None, None, None, "va", "vb", None),
            P("vb", None, "va", None),
        ),
        check_vma=False,
    )
```
